32 devices in a mesh: dp: 4 (over z), head: 2 (over x), width: 4 (over y, core).
Axes of the slice: x: 2, y: 2, z: 4, core: 2. Of those that a mesh axis runs over, the one named last changes fastest.
Arguments:
- block_in: bfloat16 [4096, 768], P('dp', ('head', 'width')), may hold values from -6 to 6
- segments: int32 [4096], P(('dp', 'head')), may hold values from 0 to 512, as said below
- live_counts: int32 [8], P('dp'), may hold values from 256 to 512, as said below
- norm1_gain: float32 [768], P(('head', 'width')), may hold values from 0.5 to 1.5
- norm1_bias: float32 [768], P(('head', 'width')), may hold values from -3 to 3
- qkv_weight: bfloat16 [768, 3, 768], P('head', None, 'width'), may hold values from -8 to 8
- qv_bias: float32 [2, 768], P(None, 'width'), may hold values from -4 to 4
- out_weight: bfloat16 [768, 768], P('width', 'head'), may hold values from -1 to 1
- out_bias: float32 [768], P(('head', 'width')), may hold values from -4 to 4
- norm2_gain: float32 [768], P(('head', 'width')), may hold values from 0.5 to 1.5
- norm2_bias: float32 [768], P(('head', 'width')), may hold values from -3 to 3
- up_weight: bfloat16 [768, 3072], P('head', 'width'), may hold values from -0.21875 to 0.21875
- up_bias: float32 [3072], P('width'), may hold values from -4 to 4
- down_weight: bfloat16 [3072, 768], P('width', 'head'), may hold values from -0.109375 to 0.109375
- down_bias: float32 [768], P(('head', 'width')), may hold values from -4 to 4
- out_cot: bfloat16 [4096, 768], P('dp', ('head', 'width')), may hold values from -6 to 6
Outputs:
- block_out: bfloat16 [4096, 768], P('dp', ('head', 'width'))
- grad_in: float32 [4096, 768], P('dp', ('head', 'width'))
- grad_norm1_gain: float32 [768], P(('head', 'width'))
- grad_norm1_bias: float32 [768], P(('head', 'width'))
- grad_qkv_weight: float32 [768, 3, 768], P('head', None, 'width')
- grad_qv_bias: float32 [2, 768], P(None, 'width')
- grad_out_weight: float32 [768, 768], P('width', 'head')
- grad_out_bias: float32 [768], P(('head', 'width'))
- grad_norm2_gain: float32 [768], P(('head', 'width'))
- grad_norm2_bias: float32 [768], P(('head', 'width'))
- grad_up_weight: float32 [768, 3072], P('head', 'width')
- grad_up_bias: float32 [3072], P('width')
- grad_down_weight: float32 [3072, 768], P('width', 'head')
- grad_down_bias: float32 [768], P(('head', 'width'))
The draws below stay inside these ranges and needn't reach their ends.
Inputs may be any that keep to these rules, and one draw needn't show every extreme that they name: `segments`: within a token block the document numbers never fall; live slots come first and carry numbers from 0 up; every slot at or past the block's live count carries 512. `live_counts`: live slots of a token block; some block is full and some holds exactly 256.
All inputs are finite; a program needn't handle non-finite values.
Results may differ from the reference program's by a relative error of at most 0.013.
Values may be sent and summed in bfloat16 or wider, within the bound.
No kernel may reach another device: no remote copies, remote signals or barrier semaphores. Data moves between devices by JAX's collectives and lax.ppermute only.
A program may use at most 64 MiB of HBM per device.

```python
import jax
import jax.numpy as jnp
from jax import lax

D = 768
FF = 3072
HD = 64
SLOTS = 512
BLOCKS = 8
TOKENS = 4096


def counts_from(key):
    base_key = jax.random.fold_in(key, 11)
    first_key, second_key = jax.random.split(base_key)
    drawn = jax.random.randint(first_key, (BLOCKS,), SLOTS // 2, SLOTS + 1)
    full_block = jax.random.randint(second_key, (), 0, BLOCKS)
    block_ids = jnp.arange(BLOCKS)
    drawn = jnp.where(block_ids == full_block, SLOTS, drawn)
    drawn = jnp.where(block_ids == (full_block + 1) % BLOCKS, SLOTS // 2, drawn)
    return drawn.astype(jnp.int32)


def draw_live_counts(key, part):
    return counts_from(key)


def draw_segments(key, part):
    lives = counts_from(key)
    start_key = jax.random.fold_in(key, 12)
    starts = jax.random.randint(start_key, (BLOCKS, SLOTS), 0, SLOTS) < 8
    positions = jnp.arange(SLOTS)[None, :]
    starts = starts | (positions == 0)
    numbers = jnp.cumsum(starts.astype(jnp.int32), axis=1) - 1
    numbers = jnp.where(positions < lives[:, None], numbers, SLOTS)
    return numbers.reshape(-1).astype(jnp.int32)


def draw_qkv_weight(key, part):
    first_key = jax.random.fold_in(jax.random.fold_in(key, 13), 0)
    drawn = jax.random.normal(first_key, (D, 3, D), jnp.float32) * D ** (-0.5)
    return jnp.clip(drawn, -8.0, 8.0).astype(jnp.bfloat16)


def block_scale(rng, extent, cuts, low, high):
    level, own = 1.0, jax.random.fold_in(rng, 6)
    for axis_at, blocks in cuts:
        draws = jnp.exp(jax.random.uniform(jax.random.fold_in(own, axis_at), (blocks,), jnp.float32, low / len(cuts), high / len(cuts)))
        level = level * jnp.repeat(draws, extent[axis_at] // blocks).reshape([-1 if axis == axis_at else 1 for axis in range(len(extent))])
    return level


def scatter_about(rng, shape, spread, bound, pieces=(), dtype=jnp.bfloat16):
    level = block_scale(rng, shape, pieces, -0.22, 0.18) if pieces else 1.0
    values = jax.random.normal(rng, shape, jnp.float32) * spread * level
    return jnp.minimum(jnp.maximum(values, -bound), bound).astype(dtype)


def setup_inputs(seed: int = 0) -> dict:
    arg_keys = jax.random.split(jax.random.key(seed), 17)
    block_in = scatter_about(arg_keys[0], (TOKENS, D), 1.0, 6.0, ((0, 4), (1, 8)))
    segments = draw_segments(jax.random.fold_in(arg_keys[16], 71), 0)
    live_counts = draw_live_counts(jax.random.fold_in(arg_keys[16], 71), 0)
    norm1_gain = jnp.clip(1.0 + 0.1 * jax.random.normal(arg_keys[3], (D,), jnp.float32), 0.5, 1.5)
    norm1_bias = scatter_about(arg_keys[4], (D,), 0.3, 3.0, ((0, 8),), jnp.float32)
    qkv_weight = draw_qkv_weight(jax.random.fold_in(arg_keys[16], 71), 0)
    qv_bias = scatter_about(arg_keys[6], (2, D), 0.5, 4.0, ((1, 4),), jnp.float32)
    out_weight = scatter_about(arg_keys[7], (D, D), (D // 24) ** -0.5, 1.0, ((0, 4), (1, 2)))
    out_bias = scatter_about(arg_keys[8], (D,), 0.5, 4.0, ((0, 8),), jnp.float32)
    norm2_gain = jnp.clip(1.0 + 0.1 * jax.random.normal(arg_keys[9], (D,), jnp.float32), 0.5, 1.5)
    norm2_bias = scatter_about(arg_keys[10], (D,), 0.3, 3.0, ((0, 8),), jnp.float32)
    up_weight = scatter_about(arg_keys[11], (D, FF), D ** -0.5, 0.21875, ((0, 2), (1, 4)))
    up_bias = scatter_about(arg_keys[12], (FF,), 0.5, 4.0, ((0, 4),), jnp.float32)
    down_weight = scatter_about(arg_keys[13], (FF, D), FF ** -0.5, 0.109375, ((0, 4), (1, 2)))
    down_bias = scatter_about(arg_keys[14], (D,), 0.5, 4.0, ((0, 8),), jnp.float32)
    out_cot = scatter_about(arg_keys[15], (TOKENS, D), 1.0, 6.0, ((0, 4), (1, 8)))
    return {"block_in": block_in, "segments": segments, "live_counts": live_counts, "norm1_gain": norm1_gain, "norm1_bias": norm1_bias, "qkv_weight": qkv_weight, "qv_bias": qv_bias, "out_weight": out_weight, "out_bias": out_bias, "norm2_gain": norm2_gain, "norm2_bias": norm2_bias, "up_weight": up_weight, "up_bias": up_bias, "down_weight": down_weight, "down_bias": down_bias, "out_cot": out_cot}


norm_eps = 1e-05

def gelu_fn(values):
    return jax.nn.gelu(values, approximate=True)

def norm_forward(rows_f, gain, shift):
    row_mean = lax.optimization_barrier(jnp.mean(rows_f, axis=1, keepdims=True))
    centred = rows_f - row_mean
    row_var = lax.optimization_barrier(jnp.mean(centred * centred, axis=1, keepdims=True))
    inv_std = lax.rsqrt(row_var + norm_eps)
    normed = centred * inv_std
    return (normed, inv_std, (normed * gain + shift).astype(jnp.bfloat16))

def norm_backward(grad_n, normed, inv_std, gain):
    scaled = grad_n * gain
    first_avg = lax.optimization_barrier(jnp.mean(scaled, axis=1, keepdims=True))
    second_avg = lax.optimization_barrier(jnp.mean(scaled * normed, axis=1, keepdims=True))
    return inv_std * (scaled - first_avg - normed * second_avg)

def reference(block_in, segments, live_counts, norm1_gain, norm1_bias, qkv_weight, qv_bias, out_weight, out_bias, norm2_gain, norm2_bias, up_weight, up_bias, down_weight, down_bias, out_cot):
    heads_all = D // HD
    scale_factor = HD ** (-0.5)
    qkv_flat = qkv_weight.reshape(D, 3 * D)
    slot_pos = jnp.arange(SLOTS).astype(jnp.int32)
    causal = slot_pos[None, :] <= slot_pos[:, None]

    def block_step(totals, item):
        rows_in, seg_rows, live_count, cot_rows = item
        rows_f = rows_in.astype(jnp.float32)
        normed1, inv1, n1_b = norm_forward(rows_f, norm1_gain, norm1_bias)
        qkv_f = jnp.dot(n1_b, qkv_flat, preferred_element_type=jnp.float32).reshape(SLOTS, 3, D)
        queries = (qkv_f[:, 0] + qv_bias[0]).astype(jnp.bfloat16).reshape(SLOTS, heads_all, HD)
        key_rows = qkv_f[:, 1].astype(jnp.bfloat16).reshape(SLOTS, heads_all, HD)
        values = (qkv_f[:, 2] + qv_bias[1]).astype(jnp.bfloat16).reshape(SLOTS, heads_all, HD)
        allowed = (seg_rows[:, None] == seg_rows[None, :]) & causal
        scores = jnp.einsum('qhd,khd->hqk', queries.astype(jnp.float32), key_rows.astype(jnp.float32)) * scale_factor
        scores = jnp.where(allowed[None], scores, -1e+30)
        peak = lax.optimization_barrier(jnp.max(scores, axis=-1, keepdims=True))
        log_total = peak + jnp.log(lax.optimization_barrier(jnp.sum(jnp.exp(scores - peak), axis=-1, keepdims=True)))
        probs_f = jnp.exp(scores - log_total)
        probs_b = probs_f.astype(jnp.bfloat16)
        mixed = jnp.einsum('hqk,khd->qhd', probs_b.astype(jnp.float32), values.astype(jnp.float32)).astype(jnp.bfloat16)
        mixed_flat = mixed.reshape(SLOTS, D)
        resid1 = rows_f + jnp.dot(mixed_flat, out_weight, preferred_element_type=jnp.float32) + out_bias
        normed2, inv2, n2_b = norm_forward(resid1, norm2_gain, norm2_bias)
        pre_act = jnp.dot(n2_b, up_weight, preferred_element_type=jnp.float32) + up_bias
        hidden = gelu_fn(pre_act).astype(jnp.bfloat16)
        result = resid1 + jnp.dot(hidden, down_weight, preferred_element_type=jnp.float32) + down_bias
        live = (slot_pos < live_count)[:, None]
        grad_out = jnp.where(live, cot_rows.astype(jnp.float32), jnp.zeros((), jnp.float32))
        grad_out_b = grad_out.astype(jnp.bfloat16)
        g_down_w = jnp.dot(hidden.T, grad_out_b, preferred_element_type=jnp.float32)
        g_down_b = lax.optimization_barrier(jnp.sum(grad_out, axis=0))
        grad_hidden = jnp.dot(grad_out_b, down_weight.T, preferred_element_type=jnp.float32)
        _, pull_back = jax.vjp(gelu_fn, pre_act)
        grad_pre = pull_back(grad_hidden)[0]
        grad_pre_b = grad_pre.astype(jnp.bfloat16)
        g_up_w = jnp.dot(n2_b.T, grad_pre_b, preferred_element_type=jnp.float32)
        g_up_b = lax.optimization_barrier(jnp.sum(grad_pre_b.astype(jnp.float32), axis=0))
        grad_n2 = jnp.dot(grad_pre_b, up_weight.T, preferred_element_type=jnp.float32)
        g_norm2_gain = lax.optimization_barrier(jnp.sum(grad_n2 * normed2, axis=0))
        g_norm2_bias = lax.optimization_barrier(jnp.sum(grad_n2, axis=0))
        grad_x1 = grad_out + norm_backward(grad_n2, normed2, inv2, norm2_gain)
        grad_x1_b = grad_x1.astype(jnp.bfloat16)
        g_out_w = jnp.dot(mixed_flat.T, grad_x1_b, preferred_element_type=jnp.float32)
        g_out_b = lax.optimization_barrier(jnp.sum(grad_x1, axis=0))
        grad_mix = jnp.dot(grad_x1_b, out_weight.T, preferred_element_type=jnp.float32).reshape(SLOTS, heads_all, HD)
        grad_mix_b = grad_mix.astype(jnp.bfloat16)
        delta = lax.optimization_barrier(jnp.sum(grad_mix * mixed.astype(jnp.float32), axis=-1)).T[:, :, None]
        grad_probs = jnp.einsum('qhd,khd->hqk', grad_mix_b.astype(jnp.float32), values.astype(jnp.float32))
        grad_scores = (probs_f * (grad_probs - delta)).astype(jnp.bfloat16).astype(jnp.float32)
        grad_q = jnp.einsum('hqk,khd->qhd', grad_scores, key_rows.astype(jnp.float32)) * scale_factor
        grad_k = jnp.einsum('hqk,qhd->khd', grad_scores, queries.astype(jnp.float32)) * scale_factor
        grad_v = jnp.einsum('hqk,qhd->khd', probs_b.astype(jnp.float32), grad_mix_b.astype(jnp.float32))
        grad_qkv = jnp.stack([grad_q, grad_k, grad_v], axis=1).reshape(SLOTS, 3 * D).astype(jnp.bfloat16)
        g_qkv_w = jnp.dot(n1_b.T, grad_qkv, preferred_element_type=jnp.float32).reshape(D, 3, D)
        column_sums = lax.optimization_barrier(jnp.sum(grad_qkv.astype(jnp.float32), axis=0)).reshape(3, D)
        g_qv_b = jnp.stack([column_sums[0], column_sums[2]], axis=0)
        grad_n1 = jnp.dot(grad_qkv, qkv_flat.T, preferred_element_type=jnp.float32)
        g_norm1_gain = lax.optimization_barrier(jnp.sum(grad_n1 * normed1, axis=0))
        g_norm1_bias = lax.optimization_barrier(jnp.sum(grad_n1, axis=0))
        grad_rows = grad_x1 + norm_backward(grad_n1, normed1, inv1, norm1_gain)
        terms = (g_norm1_gain, g_norm1_bias, g_qkv_w, g_qv_b, g_out_w, g_out_b, g_norm2_gain, g_norm2_bias, g_up_w, g_up_b, g_down_w, g_down_b)
        new_totals = tuple((total + term for total, term in zip(totals, terms)))
        return (new_totals, (result.astype(jnp.bfloat16), grad_rows))
    zeros_init = (jnp.zeros((D,), jnp.float32), jnp.zeros((D,), jnp.float32), jnp.zeros((D, 3, D), jnp.float32), jnp.zeros((2, D), jnp.float32), jnp.zeros((D, D), jnp.float32), jnp.zeros((D,), jnp.float32), jnp.zeros((D,), jnp.float32), jnp.zeros((D,), jnp.float32), jnp.zeros((D, FF), jnp.float32), jnp.zeros((FF,), jnp.float32), jnp.zeros((FF, D), jnp.float32), jnp.zeros((D,), jnp.float32))
    items = (block_in.reshape(BLOCKS, SLOTS, D), segments.reshape(BLOCKS, SLOTS), live_counts, out_cot.reshape(BLOCKS, SLOTS, D))
    totals, stacked = lax.scan(block_step, zeros_init, items)
    outputs, grads_rows = stacked
    return (outputs.reshape(TOKENS, D), grads_rows.reshape(TOKENS, D), totals[0], totals[1], totals[2], totals[3], totals[4], totals[5], totals[6], totals[7], totals[8], totals[9], totals[10], totals[11])
```

```python
import jax
import jax.numpy as jnp
from jax import lax
from jax.sharding import PartitionSpec as P

D = 768
HD = 64
EPS = 1e-05
BF = jnp.bfloat16
F32 = jnp.float32


def gelu_fn(values):
    return jax.nn.gelu(values, approximate=True)


def swap(a, dx, dy, dc):
    pairs = [
        (h * 4 + y * 2 + c, (h ^ dx) * 4 + (y ^ dy) * 2 + (c ^ dc))
        for h in range(2)
        for y in range(2)
        for c in range(2)
    ]
    return lax.ppermute(a, ("head", "width"), pairs)


def swap_dp(a, dist, size):
    return lax.ppermute(a, "dp", [(i, i ^ dist) for i in range(size)])


def pick(flag, a, b):
    return jnp.where(flag, a, b), jnp.where(flag, b, a)


def ln(v, gain, shift):
    mu = jnp.mean(v, axis=1, keepdims=True)
    cen = v - mu
    inv = lax.rsqrt(jnp.mean(cen * cen, axis=1, keepdims=True) + EPS)
    hat = cen * inv
    return hat, inv, (hat * gain + shift).astype(BF)


def dot(a, b, ca, cb):
    return lax.dot_general(a, b, (((ca,), (cb,)), ((), ())), preferred_element_type=F32)


def body(dp_size, block_in, segments, live_counts, norm1_gain, norm1_bias, qkv_weight, qv_bias,
         out_weight, out_bias, norm2_gain, norm2_bias, up_weight, up_bias, down_weight, down_bias, out_cot):
    rows = segments.shape[0]
    cols = block_in.shape[1]
    hc = qkv_weight.shape[2]
    nh = hc // HD
    h = lax.axis_index("head")
    w = lax.axis_index("width")
    d = lax.axis_index("dp")
    yf = (w // 2) == 0
    c = w % 2
    cf = c == 0
    own0 = h * rows
    oth0 = (1 - h) * rows

    def own_of(a):
        return lax.dynamic_slice_in_dim(a, own0, rows, 0)

    def oth_of(a):
        return lax.dynamic_slice_in_dim(a, oth0, rows, 0)

    def gather(own, oth):
        rx = swap(oth, 1, 0, 0)
        ry = swap(own, 0, 1, 0)
        rxy = swap(oth, 1, 1, 0)
        a0, a1 = pick(yf, own, ry)
        b0, b1 = pick(yf, rx, rxy)
        mine = jnp.concatenate([a0, a1, b0, b1], axis=1)
        other = swap(mine, 0, 0, 1)
        n = own.shape[1]
        out = []
        for i in range(4):
            sl = slice(i * n, (i + 1) * n)
            out += list(pick(cf, mine[:, sl], other[:, sl]))
        return jnp.concatenate(out, axis=1)

    vecs = jnp.stack([norm1_gain, norm1_bias, out_bias, norm2_gain, norm2_bias, down_bias, down_bias, down_bias])
    x_b = gather(own_of(block_in), oth_of(block_in))
    vec_all = gather(vecs, vecs)
    qkv_own = qkv_weight.reshape(qkv_weight.shape[0], 3 * hc)
    qkv_w = jnp.concatenate([qkv_own, swap(qkv_own, 1, 0, 0)], axis=0)
    cot_b = gather(own_of(out_cot), oth_of(out_cot))
    out_wl = jnp.concatenate([out_weight, swap(out_weight, 1, 0, 0)], axis=1)
    up_w = jnp.concatenate([up_weight, swap(up_weight, 1, 0, 0)], axis=0)
    down_w = jnp.concatenate([down_weight, swap(down_weight, 1, 0, 0)], axis=1)
    out_w2 = jnp.concatenate([out_wl, swap(out_wl, 0, 1, 0)], axis=0)
    out_wf = jnp.concatenate([out_w2, swap(out_w2, 0, 0, 1)], axis=0)
    g1, b1, ob, g2, b2, db = (vec_all[i][None, :] for i in range(6))

    x = x_b.astype(F32)
    hat1, inv1, n1 = ln(x, g1, b1)
    qkv = dot(n1, qkv_w, 1, 0)
    q = (qkv[:, :hc] + qv_bias[0]).astype(BF).reshape(rows, nh, HD)
    k = qkv[:, hc:2 * hc].astype(BF).reshape(rows, nh, HD)
    v = (qkv[:, 2 * hc:] + qv_bias[1]).astype(BF).reshape(rows, nh, HD)
    pos = jnp.arange(rows)
    allowed = (segments[:, None] == segments[None, :]) & (pos[None, :] <= pos[:, None])
    scale = HD ** (-0.5)
    s = jnp.einsum("qhd,khd->hqk", q, k, preferred_element_type=F32) * scale
    s = jnp.where(allowed[None], s, -1e30)
    peak = jnp.max(s, axis=-1, keepdims=True)
    lse = peak + jnp.log(jnp.sum(jnp.exp(s - peak), axis=-1, keepdims=True))
    p = jnp.exp(s - lse)
    pb = p.astype(BF)
    mixed = jnp.einsum("hqk,khd->qhd", pb, v, preferred_element_type=F32).astype(BF).reshape(rows, hc)
    m2 = jnp.concatenate([mixed, swap(mixed, 0, 1, 0)], axis=1)
    mf = jnp.concatenate([m2, swap(m2, 0, 0, 1)], axis=1)
    x1 = x + dot(mf, out_wf, 1, 0) + ob
    hat2, inv2, n2 = ln(x1, g2, b2)
    pre = dot(n2, up_w, 1, 0) + up_bias
    hidden, pull = jax.vjp(gelu_fn, pre)
    hidden = hidden.astype(BF)

    row_ids = jnp.arange(rows)[:, None]
    count = jnp.where(h == 0, live_counts[0], live_counts[1])
    dyb = jnp.where(row_ids < count, cot_b, jnp.zeros((), BF))
    dhid = dot(dyb, down_w, 1, 1)
    dpre = pull(dhid)[0].astype(BF)
    dn2p = dot(dpre, up_w, 1, 1)
    half = rows // 2
    keep = lax.dynamic_slice_in_dim(dn2p, c * half, half, 0)
    give = lax.dynamic_slice_in_dim(dn2p, (1 - c) * half, half, 0)
    chip = (keep + swap(give.astype(BF), 0, 0, 1).astype(F32)).astype(BF)
    dn2 = chip.astype(F32) + swap(chip, 0, 1, 0).astype(F32)
    hat2h = lax.dynamic_slice_in_dim(hat2, c * half, half, 0)
    inv2h = lax.dynamic_slice_in_dim(inv2, c * half, half, 0)
    dyh = lax.dynamic_slice_in_dim(dyb, c * half, half, 0)
    sc = dn2 * g2
    dx1h = dyh.astype(F32) + inv2h * (
        sc - jnp.mean(sc, axis=1, keepdims=True) - hat2h * jnp.mean(sc * hat2h, axis=1, keepdims=True))
    dx1hb = dx1h.astype(BF)
    lo, hi = pick(cf, dx1hb, swap(dx1hb, 0, 0, 1))
    dx1b = jnp.concatenate([lo, hi], axis=0)

    dmix = dot(dx1b, out_wl, 1, 1)
    dmixb = dmix.astype(BF).reshape(rows, nh, HD)
    delta = jnp.sum((dmix * mixed.astype(F32)).reshape(rows, nh, HD), axis=-1).T[:, :, None]
    dpr = jnp.einsum("qhd,khd->hqk", dmixb, v, preferred_element_type=F32)
    ds = (p * (dpr - delta)).astype(BF)
    dv = jnp.einsum("hqk,qhd->khd", pb, dmixb, preferred_element_type=F32)
    dk = jnp.einsum("hqk,qhd->khd", ds, q, preferred_element_type=F32) * scale
    dq = jnp.einsum("hqk,khd->qhd", ds, k, preferred_element_type=F32) * scale
    dqkv = jnp.stack([dq, dk, dv], axis=1).reshape(rows, 3 * hc).astype(BF)
    dn1p = dot(dqkv, qkv_w, 1, 1)
    sc1 = dn1p * g1
    st = jnp.stack([jnp.sum(sc1, axis=1), jnp.sum(sc1 * hat1, axis=1)])
    st = st + swap(st, 0, 0, 1)
    st = st + swap(st, 0, 1, 0)
    st = st / D

    def pieces(a):
        return [[lax.dynamic_slice_in_dim(a, dx * 4 * cols + (w ^ dw) * cols, cols, 1) for dw in range(4)]
                for dx in range(2)]

    def to_owner(partial, extra):
        pp, ee = pieces(partial), pieces(extra)
        send = jnp.concatenate([pp[0][1], pp[1][1], pp[0][3], pp[1][3]], axis=1).astype(BF)
        got = swap(send, 0, 0, 1).astype(F32)
        g = [got[:, i * cols:(i + 1) * cols] for i in range(4)]
        own = pp[0][0] + g[0] + ee[0][0]
        sx = (pp[1][0] + g[1] + ee[1][0]).astype(BF)
        sy = (pp[0][2] + g[2]).astype(BF)
        sxy = (pp[1][2] + g[3]).astype(BF)
        rx = swap(sx, 1, 0, 0).astype(F32)
        ry = swap(sy, 0, 1, 0).astype(F32)
        rxy = swap(sxy, 1, 1, 0).astype(F32)
        a, b = own + ry, rx + rxy
        return jnp.concatenate(list(pick(h == 0, a, b)), axis=0)

    y_out = to_owner(dot(hidden, down_w, 1, 0), x1 + db).astype(BF)
    scale_in = inv1 * g1
    gi_extra = dx1b.astype(F32) - inv1 * (st[0][:, None] + hat1 * st[1][:, None])
    grad_in = to_owner(dn1p * scale_in, gi_extra)

    def x_reduce(own, oth):
        return own + swap(oth.astype(BF), 1, 0, 0).astype(F32)

    def dp_reduce(g):
        n = g.shape[0] // 2
        b = d % 2
        kp = lax.dynamic_slice_in_dim(g, b * n, n, 0)
        gv = lax.dynamic_slice_in_dim(g, (1 - b) * n, n, 0)
        sm = (kp + swap_dp(gv.astype(BF), 1, dp_size).astype(F32)).astype(BF)
        dist = 2
        while dist < dp_size:
            sm = (sm.astype(F32) + swap_dp(sm, dist, dp_size).astype(F32)).astype(BF)
            dist *= 2
        return jnp.concatenate(list(pick(b == 0, sm, swap_dp(sm, 1, dp_size))), axis=0).astype(F32)

    def dp_sum(g):
        dist = 1
        while dist < dp_size:
            g = g + swap_dp(g, dist, dp_size)
            dist *= 2
        return g

    half_d = D // 2
    gd = dot(hidden, dyb, 0, 0)
    g_down_w = dp_reduce(x_reduce(gd[:, :half_d], gd[:, half_d:]))
    gu = dot(n2, dpre, 0, 0)
    g_up_w = dp_reduce(x_reduce(gu[:half_d], gu[half_d:]))
    go = dot(mixed, dx1b, 0, 0)
    g_out_w = dp_reduce(x_reduce(go[:, :half_d], go[:, half_d:]))
    gq = dot(n1, dqkv, 0, 0)
    g_qkv_w = dp_reduce(x_reduce(gq[:half_d], gq[half_d:])).reshape(qkv_weight.shape)

    n2v = jnp.stack([jnp.sum(dn2 * hat2h, axis=0), jnp.sum(dn2, axis=0), jnp.sum(dx1h, axis=0)])
    n2v = n2v + swap(n2v, 0, 0, 1)
    dq_sum = jnp.sum(dqkv.astype(F32), axis=0)
    up_b = jnp.sum(dpre.astype(F32), axis=0)
    qv_sum = jnp.concatenate([dq_sum[:hc], dq_sum[2 * hc:]])
    n2x = n2v[:, :half_d] + swap(n2v[:, half_d:], 1, 0, 0)
    lv = jnp.concatenate([up_b, qv_sum])
    lv = lv + swap(lv, 1, 0, 0)
    n2w = lax.dynamic_slice_in_dim(n2x, w * cols, cols, 1)
    dy_sum = jnp.sum(dyb.astype(F32), axis=0)
    dyx = dy_sum[:half_d] + swap(dy_sum[half_d:], 1, 0, 0)
    dyw = lax.dynamic_slice_in_dim(dyx, w * cols, cols, 0)
    dn1_sum = jnp.stack([jnp.sum(dn1p * hat1, axis=0), jnp.sum(dn1p, axis=0)])
    dn1_sum = dn1_sum + swap(dn1_sum, 0, 0, 1)
    dn1_sum = dn1_sum + swap(dn1_sum, 0, 1, 0)
    dn1_x = dn1_sum[:, :half_d] + swap(dn1_sum[:, half_d:], 1, 0, 0)
    dn1_w = lax.dynamic_slice_in_dim(dn1_x, w * cols, cols, 1)
    tail = jnp.concatenate([n2w.reshape(-1), dyw, dn1_w.reshape(-1), lv])
    tail = dp_sum(tail)
    g_n2g, g_n2b, g_ob, g_db, g_n1g, g_n1b = (tail[i * cols:(i + 1) * cols] for i in range(6))
    rest = tail[6 * cols:]
    ffl = up_bias.shape[0]
    g_ub = rest[:ffl]
    g_qv = rest[ffl:].reshape(2, hc)
    return (y_out, grad_in, g_n1g, g_n1b, g_qkv_w, g_qv, g_out_w, g_ob, g_n2g, g_n2b, g_up_w, g_ub,
            g_down_w, g_db)


def solution(mesh):
    dp_size = mesh.shape["dp"]
    hw = ("head", "width")

    def run(*args):
        return body(dp_size, *args)

    return jax.shard_map(
        run,
        mesh=mesh,
        in_specs=(
            P("dp", hw), P(("dp", "head")), P("dp"), P(hw), P(hw), P("head", None, "width"),
            P(None, "width"), P("width", "head"), P(hw), P(hw), P(hw), P("head", "width"),
            P("width"), P("width", "head"), P(hw), P("dp", hw),
        ),
        out_specs=(
            P("dp", hw), P("dp", hw), P(hw), P(hw), P("head", None, "width"), P(None, "width"),
            P("width", "head"), P(hw), P(hw), P(hw), P("head", "width"), P("width"),
            P("width", "head"), P(hw),
        ),
        check_vma=False,
    )
```

```python
import jax
import jax.numpy as jnp
from jax import lax
from jax.experimental import pallas as pl
from jax.experimental.pallas import tpu as pltpu
from jax.sharding import PartitionSpec as P


HD = 64
EPS = 1e-05
BF = jnp.bfloat16
F32 = jnp.float32
T = 512
HALF = 384
D = 768
C1 = 0.7978845608028654
C2 = 0.044715


def sds(shape, dtype):
    return jax.ShapeDtypeStruct(shape, dtype)


def kernel_call(fn, outs, *args, scratch=(), vmem=22, own=False, out=False):
    space = pltpu.HBM if own else pltpu.VMEM
    small = [a.dtype == jnp.int32 for a in args]
    specs = [pl.BlockSpec(memory_space=pltpu.SMEM if m else space) for m in small]
    n, extra, run = len(args) - 1, [], fn
    if own:
        extra = [pltpu.VMEM(a.shape, a.dtype) for a in args[1:]] + [pltpu.SemaphoreType.DMA((n,))]

        def run(m, *refs):
            k = n + len(outs)
            bufs, sems, rest = refs[k:k + n], refs[k + n], refs[k + n + 1:]
            copies = [pltpu.make_async_copy(refs[i], bufs[i], sems.at[i]) for i in range(n)]
            for cp in copies:
                cp.start()
            for cp in copies:
                cp.wait()
            fn(m, *bufs, *refs[n:k], *rest)
    elif out:
        q = len(outs)
        extra = [pltpu.VMEM(*o) for o in outs] + [pltpu.SemaphoreType.DMA((q,))]

        def run(m, *refs):
            k = n + q
            bufs, sems, rest = refs[k:k + q], refs[k + q], refs[k + q + 1:]
            fn(m, *refs[:n], *bufs, *rest)
            copies = [pltpu.make_async_copy(bufs[i], refs[n + i], sems.at[i]) for i in range(q)]
            for cp in copies:
                cp.start()
            for cp in copies:
                cp.wait()

    return pl.pallas_call(
        run,
        out_shape=[sds(*o) for o in outs],
        in_specs=specs,
        out_specs=[pl.BlockSpec(memory_space=pltpu.HBM if out else pltpu.VMEM)] * len(outs),
        scratch_shapes=extra + list(scratch),
        compiler_params=pltpu.CompilerParams(vmem_limit_bytes=vmem << 20),
    )(*args)


def nn(a, b):
    return lax.dot_general(a, b, (((1,), (0,)), ((), ())), preferred_element_type=F32)


def tn(a, b):
    return lax.dot_general(a, b, (((0,), (0,)), ((), ())), preferred_element_type=F32)


def nt(a, b):
    return lax.dot_general(a, b, (((1,), (1,)), ((), ())), preferred_element_type=F32)


def rnd(a):
    return a.astype(BF).astype(F32)


def ds(start, size):
    return pl.ds(pl.multiple_of(start, 32), size)


def own_slots(i):
    h = lax.axis_index("head")
    blk = h if i == 0 else 1 - h
    return blk, pl.ds(pl.multiple_of(blk * T, T), T)


def k_pack(xin, vin, xo, xt):
    eye = (lax.broadcasted_iota(jnp.int32, (96, 96), 0) == lax.broadcasted_iota(jnp.int32, (96, 96), 1)).astype(
        F32).astype(BF)
    v = vin[...]
    hi = rnd(v)
    vv = jnp.concatenate([hi, v - hi, jnp.zeros((112, 96), F32)], axis=0)
    vc = nt(eye, vv.astype(BF)).astype(BF)
    for i, xr in enumerate((xo, xt)):
        xr[:, :T] = xin[:, own_slots(i)[1]]
        xr[:, T:] = vc


def k_cot(meta, cin, co, ct, dbs):
    lane = lax.broadcasted_iota(jnp.int32, (96, T), 1)
    tot = jnp.zeros((96, 1), F32)
    for i, cr in enumerate((co, ct)):
        blk, slots = own_slots(i)
        cnt = jnp.where(blk == 0, meta[3], meta[4])
        c = jnp.where(lane < cnt, cin[:, slots].astype(F32), 0.0)
        cr[...] = c.astype(BF)
        tot = tot + jnp.sum(c, axis=1, keepdims=True)
    dbs[...] = jnp.broadcast_to(tot, (96, 128))


def place(meta, mine, other, dst, width, lane0=0):
    y, c = meta[1], meta[2]
    for dx in range(2):
        for dy in range(2):
            src = (dx * 2 + dy) * 96
            base = dx * HALF + (y if dy == 0 else 1 - y) * 192
            dst[ds(base + c * 96, 96), :] = mine[src:src + 96, lane0:lane0 + width].astype(dst.dtype)
            dst[ds(base + (1 - c) * 96, 96), :] = other[src:src + 96, lane0:lane0 + width].astype(dst.dtype)


def layer_norm(x):
    mu = jnp.mean(x, axis=0, keepdims=True)
    cen = x - mu
    inv = lax.rsqrt(jnp.mean(cen * cen, axis=0, keepdims=True) + EPS)
    return cen * inv, mu, inv


def allowed_mask(seg_row, nk, q0):
    seg_col = jnp.transpose(jnp.broadcast_to(seg_row, (128, T)))[:nk, :1]
    kk = lax.broadcasted_iota(jnp.int32, (nk, 256), 0)
    qq = lax.broadcasted_iota(jnp.int32, (nk, 256), 1) + q0
    return (seg_col == seg_row[:, q0:q0 + 256]) & (kk <= qq)


def k_attn(meta, mine, other, wo, wr, qvb, seg, xT, n1T, vec, st, qkvT, mixT, xs, vs):
    nf = wo.shape[0]
    hc = nf // 3
    place(meta, mine, other, xs, T)
    place(meta, mine, other, vs, 128, T)
    v = vs[:, 0:8] + vs[:, 8:16]
    vec[...] = v
    x = xs[...]
    xT[...] = x.astype(BF)
    hat, mu, inv = layer_norm(x)
    n1 = (hat * v[:, 0:1] + v[:, 1:2]).astype(BF)
    n1T[...] = n1
    qkv = nn(wo[...], n1[:HALF]) + nn(wr[...], n1[HALF:])
    b = qvb[...]
    q = (qkv[:hc] + b[:, 0:1]).astype(BF)
    k = qkv[hc:2 * hc].astype(BF)
    vv = (qkv[2 * hc:] + b[:, 1:2]).astype(BF)
    qkvT[0:hc] = q
    qkvT[hc:2 * hc] = k
    qkvT[2 * hc:] = vv
    st[...] = jnp.concatenate([mu, inv, jnp.zeros((6, T), F32)], axis=0)
    seg_row = seg[...]
    for jq in range(2):
        nk = (jq + 1) * 256
        ok = allowed_mask(seg_row, nk, jq * 256)
        for j in range(hc // HD):
            r = slice(j * HD, (j + 1) * HD)
            s = tn(k[r, :nk], q[r, jq * 256:nk]) * (HD ** -0.5)
            s = jnp.where(ok, s, -1e30)
            m = jnp.max(s, axis=0, keepdims=True)
            e = jnp.exp(s - m)
            l = jnp.sum(e, axis=0, keepdims=True)
            st[2 + j:3 + j, jq * 256:nk] = m + jnp.log(l)
            pb = (e * (1.0 / l)).astype(BF)
            mixT[r, jq * 256:nk] = nn(vv[r, :nk], pb).astype(BF)


def k_mlp(meta, xT, vec, ma, mb, mc, md, woa, wob, uo, ur, do, d0, d1, d2, d3, ub, cm, co,
          keep, give, hT, dpT, n2T, x1T, st2, dyT, dr, hats):
    c = meta[2]
    n = d0.shape[0]
    for i, r in enumerate((d0, d1, d2, d3)):
        dr[ds((meta[5] ^ i) * n, n), :] = r[...]
    v = vec[...]
    hc = ma.shape[0]
    parts = []
    for dx in range(2):
        acc = None
        for ms, w in (((ma, mb), woa), ((mc, md), wob)):
            for dy in range(2):
                t = tn(w[(dy * 2 + dx) * hc:(dy * 2 + dx + 1) * hc, :], ms[dy][...])
                acc = t if acc is None else acc + t
        r = slice(dx * HALF, (dx + 1) * HALF)
        parts.append(xT[r, :].astype(F32) + acc + v[r, 2:3])
    x1 = jnp.concatenate(parts, axis=0)
    x1T[...] = x1
    hat, mu, inv = layer_norm(x1)
    st2[...] = jnp.concatenate([mu, inv, jnp.zeros((6, T), F32)], axis=0)
    n2 = (hat * v[:, 3:4] + v[:, 4:5]).astype(BF)
    n2T[...] = n2
    place(meta, cm, co, dyT, T)
    dy = dyT[...]
    dhid = nn(do[...], dy[:HALF]) + nn(dr[...], dy[HALF:])
    p = tn(uo[...], n2[:HALF]) + tn(ur[...], n2[HALF:]) + ub[:, 0:1]
    p2 = p * p
    t = jnp.tanh(C1 * (p + C2 * p * p2))
    hT[...] = (0.5 * p * (1.0 + t)).astype(BF)
    dpre = dhid * (0.5 * (1.0 + t) + 0.5 * p * (1.0 - t * t) * (C1 * (1.0 + 3.0 * C2 * p2)))
    dp = dpre.astype(BF)
    dpT[...] = dp
    for dx, w in ((0, uo), (1, ur)):
        hats[dx * HALF:(dx + 1) * HALF, :] = nn(w[...], dp)
    keep[...] = hats[:, pl.ds(pl.multiple_of(c * 256, 256), 256)]
    give[...] = hats[:, pl.ds(pl.multiple_of((1 - c) * 256, 256), 256)].astype(BF)


def split_pieces(meta, src, extra, keep, give):
    y, c = meta[1], meta[2]
    for dy in range(2):
        for dx in range(2):
            i = (dy * 2 + dx) * 96
            base = dx * HALF + (y if dy == 0 else 1 - y) * 192
            a = src[ds(base + c * 96, 96), :]
            g = src[ds(base + (1 - c) * 96, 96), :]
            if extra is not None and dy == 0:
                a = a + extra[ds(base + c * 96, 96), :]
            keep[i:i + 96, :] = a
            give[i:i + 96, :] = g.astype(BF)


def rows_of(b, n):
    return pl.ds(pl.multiple_of(b * n, 16), n)


def k_down_grad(meta, hT, dyT, keep, gx, gz, gxz):
    b = meta[6]
    n = hT.shape[0] // 2
    mine, his = hT[rows_of(b, n), :], hT[rows_of(1 - b, n), :]
    o, t = dyT[:HALF], dyT[HALF:]
    gx[...] = nt(mine, t).astype(BF)
    gz[...] = nt(his, o).astype(BF)
    gxz[...] = nt(his, t).astype(BF)
    keep[...] = nt(mine, o)


def k_up_grad(meta, dpT, n2T, hT, do, dr, x1T, vec, keep, gx, gz, gxz, yk, yg, ys, xd):
    b = meta[6]
    n = dpT.shape[0] // 2
    ones = jnp.ones((16, T), BF)
    mine, his = dpT[rows_of(b, n), :], dpT[rows_of(1 - b, n), :]
    o, t = n2T[:HALF], n2T[HALF:]
    sm, sh = nt(ones, mine), nt(ones, his)
    for ref, rows, units, sums in ((gxz, t, his, sh), (gz, o, his, sh), (gx, t, mine, sm), (keep, o, mine, sm)):
        ref[:HALF, :] = nt(rows, units).astype(ref.dtype)
        ref[HALF:, :] = sums.astype(ref.dtype)
    ys[:HALF, :] = tn(do[...], hT[...])
    ys[HALF:, :] = tn(dr[...], hT[...])
    xd[...] = x1T[...] + vec[:, 5:6]
    split_pieces(meta, ys, xd, yk, yg)


def k_ln2_back(meta, chip, recv, x1T, st2, dyT, vec, dm):
    c = meta[2]
    half = pl.ds(pl.multiple_of(c * 256, 256), 256)
    dn2 = chip[...].astype(F32) + recv[...].astype(F32)
    mu = st2[0:1, half]
    inv = st2[1:2, half]
    hat = (x1T[:, half] - mu) * inv
    sc = dn2 * vec[:, 3:4]
    m1 = jnp.mean(sc, axis=0, keepdims=True)
    m2 = jnp.mean(sc * hat, axis=0, keepdims=True)
    dx1 = dyT[:, half].astype(F32) + inv * (sc - m1 - hat * m2)
    dm[:, :256] = dx1.astype(BF)
    lane = lax.broadcasted_iota(jnp.int32, (D, 128), 1)
    s0 = jnp.sum(dn2 * hat, axis=1, keepdims=True)
    s1 = jnp.sum(dn2, axis=1, keepdims=True)
    s2 = jnp.sum(dx1, axis=1, keepdims=True)
    dm[:, 256:] = jnp.where(lane == 0, s0, jnp.where(lane == 1, s1, jnp.where(lane == 2, s2, 0.0))).astype(BF)


def k_attn_back(meta, dm, dmo, wa, mixT, qkvT, st, seg, wo, wr, xT, vec,
                dx1T, dqkvT, keep, kst, give, acc, dn):
    c = meta[2]
    hc = mixT.shape[0]
    dx1T[:, pl.ds(pl.multiple_of(c * 256, 256), 256)] = dm[:, :256]
    dx1T[:, pl.ds(pl.multiple_of((1 - c) * 256, 256), 256)] = dmo[:, :256]
    dmix = nn(wa[:hc, :], dx1T[:HALF, :]) + nn(wa[hc:2 * hc, :], dx1T[HALF:, :])
    dmb = dmix.astype(BF)
    dl = dmix * mixT[...].astype(F32)
    seg_row = seg[...]
    sc = HD ** -0.5
    for jq in (1, 0):
        q0, nk = jq * 256, (jq + 1) * 256
        ok = allowed_mask(seg_row, nk, q0)
        for j in range(hc // HD):
            r = slice(j * HD, (j + 1) * HD)
            rk = slice(hc + j * HD, hc + (j + 1) * HD)
            rv = slice(2 * hc + j * HD, 2 * hc + (j + 1) * HD)
            qc = qkvT[r, q0:nk]
            kc = qkvT[rk, :nk]
            s = tn(kc, qc) * sc
            p = jnp.where(ok, jnp.exp(jnp.where(ok, s, -1e30) - st[2 + j:3 + j, q0:nk]), 0.0)
            dpr = tn(qkvT[rv, :nk], dmb[r, q0:nk])
            delta = jnp.sum(dl[r, q0:nk], axis=0, keepdims=True)
            dsb = (p * (dpr - delta)).astype(BF)
            dqkvT[r, q0:nk] = (nn(kc, dsb) * sc).astype(BF)
            dk = nt(qc, dsb) * sc
            dv = nt(dmb[r, q0:nk], p.astype(BF))
            if jq == 1:
                acc[r, :] = dk
                acc[rk, :] = dv
            else:
                acc[r, :256] = acc[r, :256] + dk
                acc[rk, :256] = acc[rk, :256] + dv
    dqkvT[hc:2 * hc, :] = acc[:hc, :].astype(BF)
    dqkvT[2 * hc:, :] = acc[hc:, :].astype(BF)
    s1 = jnp.zeros((1, T), F32)
    s2 = jnp.zeros((1, T), F32)
    mu = st[0:1, :]
    inv = st[1:2, :]
    for dx, w in ((0, wo), (1, wr)):
        r = slice(dx * HALF, (dx + 1) * HALF)
        dn1 = tn(w[...], dqkvT[...])
        dn[r, :] = dn1
        g = dn1 * vec[r, 0:1]
        s1 = s1 + jnp.sum(g, axis=0, keepdims=True)
        s2 = s2 + jnp.sum(g * (xT[r, :].astype(F32) - mu) * inv, axis=0, keepdims=True)
    split_pieces(meta, dn, None, keep, give)
    kst[...] = jnp.concatenate([s1, s2, jnp.zeros((6, T), F32)], axis=0)
    give[HALF:, :] = stat_rows(s1, s2)


def stat_rows(s1, s2):
    h1, h2 = rnd(s1), rnd(s2)
    return jnp.concatenate([h1, s1 - h1, h2, s2 - h2, jnp.zeros((12, T), F32)], axis=0).astype(BF)


def k_qkv_grad(meta, n1T, dqkvT, keep, his, gx):
    b = meta[6]
    n = dqkvT.shape[0] // 2
    o, t = n1T[:HALF], n1T[HALF:]
    for i, ref in ((0, keep), (1, his)):
        q = dqkvT[rows_of(b if i == 0 else 1 - b, n), :]
        gx[i * n:(i + 1) * n, :] = nt(q, t).astype(BF)
        ref[...] = nt(q, o)


def k_out_grad(meta, mixT, dx1T, dm, dmo, dqkvT, keep, his, gx):
    b = meta[6]
    hc = mixT.shape[0]
    n = hc // 2
    ones = jnp.ones((16, T), BF)
    sv = jnp.transpose(dm[:, 256:].astype(F32) + dmo[:, 256:].astype(F32))[:16]
    low = lax.broadcasted_iota(jnp.int32, (8, hc), 0) < 4
    sums = jnp.where(low, nt(ones, dqkvT[:hc])[:8], nt(ones, dqkvT[2 * hc:])[:8])
    zero = jnp.zeros((8, HALF - hc), F32)
    sums = jnp.concatenate([sums, zero], axis=1)
    m = n + 16
    for i, ref in ((0, keep), (1, his)):
        x = mixT[rows_of(b if i == 0 else 1 - b, n), :]
        gx[i * m:i * m + n, :] = nt(x, dx1T[HALF:, :]).astype(BF)
        gx[i * m + n:(i + 1) * m, :] = jnp.concatenate([sv[:8, HALF:], sums], axis=0).astype(BF)
        ref[:n, :] = nt(x, dx1T[:HALF, :])
        ref[n:, :] = jnp.concatenate([sv[:8, :HALF], sums], axis=0)


def k_vectors(meta, own, other, v, n1g, n1b, ob, n2g, n2b, db, qv):
    first = meta[6] == 0
    w = meta[1] * 2 + meta[2]
    n = own.shape[0] - 16
    a = jnp.where(first, own[n:, :].astype(F32), other[n:, :].astype(F32))
    g = jnp.zeros((8, 96), F32)
    for i in range(4):
        g = jnp.where(w == i, a[:8, i * 96:(i + 1) * 96], g)
    n2g[...] = g[0:1]
    n2b[...] = g[1:2]
    ob[...] = g[2:3]
    hc = qv.shape[1]
    qv[0:1, :] = a[8:9, :hc]
    qv[1:2, :] = a[12:13, :hc]
    n1g[...] = v[0:1, :96]
    n1b[...] = v[1:2, :96]
    db[...] = v[2:3, :96]


def k_chip(meta, keep, kst, got, own, ost, send):
    a = keep[...] + got[:HALF, :].astype(F32)
    own[...] = a[:192]
    send[:192, :] = a[192:].astype(BF)
    g = got[HALF:, :].astype(F32)
    s1 = kst[0:1, :] + g[0:1] + g[1:2]
    s2 = kst[1:2, :] + g[2:3] + g[3:4]
    ost[...] = jnp.concatenate([s1, s2, jnp.zeros((6, T), F32)], axis=0)
    send[192:, :] = stat_rows(s1, s2)


def k_grad_in(meta, own, ost, got, xT, st, dx1T, vec, mine, sums, send):
    y, c = meta[1], meta[2]
    g = got[192:, :].astype(F32)
    m1 = (ost[0:1, :] + g[0:1] + g[1:2]) / D
    m2 = (ost[1:2, :] + g[2:3] + g[3:4]) / D
    mu, inv = st[0:1, :], st[1:2, :]
    lane = lax.broadcasted_iota(jnp.int32, (96, 128), 1)
    for dx in range(2):
        i = dx * 96
        rows = ds(dx * HALF + y * 192 + c * 96, 96)
        dn1 = own[i:i + 96, :] + got[i:i + 96, :].astype(F32)
        hat = (xT[rows, :].astype(F32) - mu) * inv
        gi = dx1T[rows, :].astype(F32) + inv * (dn1 * vec[rows, 0:1] - m1 - hat * m2)
        s0 = jnp.sum(dn1 * hat, axis=1, keepdims=True)
        s1 = jnp.sum(dn1, axis=1, keepdims=True)
        sv = jnp.where(lane == 0, s0, jnp.where(lane == 1, s1, 0.0))
        if dx == 0:
            mine[...] = gi
            sums[...] = sv
        else:
            send[:, :T] = gi.astype(BF)
            send[:, T:] = sv.astype(BF)


def k_final(meta, mine, sums, got, dbs, ym, yo, grad_in, yout, vsum):
    h = meta[0]
    lane = lax.broadcasted_iota(jnp.int32, (96, 128), 1)
    v = jnp.where(lane == 2, dbs[...], sums[...] + got[:, T:].astype(F32))
    vsum[...] = jnp.transpose(jnp.concatenate([v, jnp.zeros((32, 128), F32)], axis=0))[:8]
    own = pl.ds(pl.multiple_of(h * T, T), T)
    oth = pl.ds(pl.multiple_of((1 - h) * T, T), T)
    grad_in[:, own] = mine[...]
    grad_in[:, oth] = got[:, :T].astype(F32)
    yout[:, own] = ym[...].astype(BF)
    yout[:, oth] = yo[...]


def pick(flag, a, b):
    return jnp.where(flag, a, b), jnp.where(flag, b, a)


def swap(a, dx, dy, dc):
    pairs = [
        (h * 4 + y * 2 + c, (h ^ dx) * 4 + (y ^ dy) * 2 + (c ^ dc))
        for h in range(2)
        for y in range(2)
        for c in range(2)
    ]
    return lax.ppermute(a, ("head", "width"), pairs)


def swap_dp(a, dist, size):
    return lax.ppermute(a, "dp", [(i, i ^ dist) for i in range(size)])


def body(dp_size, block_in, segments, live_counts, norm1_gain, norm1_bias, qkv_weight, qv_bias,
         out_weight, out_bias, norm2_gain, norm2_bias, up_weight, up_bias, down_weight, down_bias, out_cot):
    hc = qkv_weight.shape[2]
    ff = up_weight.shape[1]
    h = lax.axis_index("head")
    w = lax.axis_index("width")
    d = lax.axis_index("dp")
    meta = jnp.stack([h, w // 2, w % 2, live_counts[0], live_counts[1], d % 4, d % 2]).astype(jnp.int32)

    vecs = jnp.stack([norm1_gain, norm1_bias, out_bias, norm2_gain, norm2_bias, down_bias, down_bias, down_bias])
    xo, xt = kernel_call(k_pack, [((96, 640), BF), ((96, 640), BF)], block_in.T, vecs)
    cot_o, cot_t, dbs = kernel_call(
        k_cot, [((96, T), BF), ((96, T), BF), ((96, 128), F32)], meta, out_cot.T)
    rx = swap(xt, 1, 0, 0)
    rxy = swap(xt, 1, 1, 0)
    ry = swap(xo, 0, 1, 0)
    wq_o = qkv_weight.transpose(1, 2, 0).reshape(3 * hc, HALF)
    wout_r = swap(out_weight, 1, 0, 0)
    quarter = ff // 4
    wd0 = swap(lax.dynamic_slice_in_dim(down_weight, (d % 4) * quarter, quarter, 0), 1, 0, 0)
    wq_r = swap(wq_o, 1, 0, 0)
    xm = jnp.concatenate([xo, ry, rx, rxy], axis=0)
    xc = swap(xm, 0, 0, 1)
    cot_y = swap(jnp.concatenate([cot_o, cot_t], axis=0), 0, 1, 0)
    cot_x = swap(jnp.concatenate([cot_t, cot_y[96:]], axis=0), 1, 0, 0)
    wu_r = swap(up_weight, 1, 0, 0)
    wd1, wd2, wd3 = (swap_dp(wd0, i, dp_size) for i in (1, 2, 3))
    woa2 = jnp.concatenate([out_weight, wout_r], axis=0)
    woa = jnp.concatenate([woa2, swap(woa2, 0, 1, 0)], axis=0)
    wob = swap(woa, 0, 0, 1)
    qvb = jnp.concatenate([qv_bias, jnp.zeros((6, hc), F32)], axis=0).T
    ub = jnp.broadcast_to(up_bias[:, None], (ff, 8))
    seg = segments.astype(F32)[None, :]
    cm = jnp.concatenate([cot_o, cot_y[:96], cot_x], axis=0)
    cc = swap(cm, 0, 0, 1)

    xT, n1T, vec, st, qkvT, mixT = kernel_call(
        k_attn,
        [((D, T), BF), ((D, T), BF), ((D, 8), F32), ((8, T), F32), ((3 * hc, T), BF), ((hc, T), BF)],
        meta, xm, xc, wq_o, wq_r, qvb, seg,
        scratch=[pltpu.VMEM((D, T), F32), pltpu.VMEM((D, 128), F32)], own=True)
    mix_y = swap(mixT, 0, 1, 0)
    mixes = [mixT, mix_y, swap(mixT, 0, 0, 1), swap(mix_y, 0, 0, 1)]

    keep, give, hT, dpT, n2T, x1T, st2, dyT, wd_r = kernel_call(
        k_mlp,
        [((D, 256), F32), ((D, 256), BF), ((ff, T), BF), ((ff, T), BF), ((D, T), BF), ((D, T), F32), ((8, T), F32),
         ((D, T), BF), ((ff, HALF), BF)],
        meta, xT, vec, *mixes, woa, wob, up_weight, wu_r, down_weight, wd0, wd1, wd2, wd3, ub, cm, cc,
        scratch=[pltpu.VMEM((D, T), F32)])
    chip = (keep + swap(give, 0, 0, 1).astype(F32)).astype(BF)
    chip_r = swap(chip, 0, 1, 0)
    half_ff = ff // 2
    gd4 = kernel_call(
        k_down_grad,
        [((half_ff, HALF), F32)] + [((half_ff, HALF), BF)] * 3, meta, hT, dyT)
    m = HALF + 16
    *gu4, yk, yg = kernel_call(
        k_up_grad,
        [((m, half_ff), F32)] + [((m, half_ff), BF)] * 3 + [((HALF, T), F32), ((HALF, T), BF)],
        meta, dpT, n2T, hT, down_weight, wd_r, x1T, vec,
        scratch=[pltpu.VMEM((D, T), F32), pltpu.VMEM((D, T), F32)])
    ychip = yk + swap(yg, 0, 0, 1).astype(F32)
    yr = ychip[:192] + swap(ychip[192:].astype(BF), 0, 1, 0).astype(F32)
    yo = swap(yr[96:].astype(BF), 1, 0, 0)
    ym = yr[:96]

    dm, = kernel_call(k_ln2_back, [((D, 384), BF)], meta, chip, chip_r, x1T, st2, dyT, vec)
    dmo = swap(dm, 0, 0, 1)
    dx1T, dqkvT, keep1, kst, give1 = kernel_call(
        k_attn_back,
        [((D, T), BF), ((3 * hc, T), BF), ((HALF, T), F32), ((8, T), F32), ((HALF + 16, T), BF)],
        meta, dm, dmo, woa2, mixT, qkvT, st, seg, wq_o, wq_r, xT, vec,
        scratch=[pltpu.VMEM((2 * hc, T), F32), pltpu.VMEM((D, T), F32)])
    got1 = swap(give1, 0, 0, 1)
    m = 3 * hc // 2
    gq3 = kernel_call(
        k_qkv_grad, [((m, HALF), F32), ((m, HALF), F32), ((2 * m, HALF), BF)], meta, n1T, dqkvT)
    m = hc // 2 + 16
    go3 = kernel_call(
        k_out_grad, [((m, HALF), F32), ((m, HALF), F32), ((2 * m, HALF), BF)],
        meta, mixT, dx1T, dm, dmo, dqkvT)
    own1, ost, send1 = kernel_call(
        k_chip, [((192, T), F32), ((8, T), F32), ((208, T), BF)], meta, keep1, kst, got1)
    got2 = swap(send1, 0, 1, 0)
    mine, sums, send2 = kernel_call(
        k_grad_in, [((96, T), F32), ((96, 128), F32), ((96, 640), BF)],
        meta, own1, ost, got2, xT, st, dx1T, vec)
    got3 = swap(send2, 1, 0, 0)
    grad_in, y_out, vsum = kernel_call(
        k_final, [((96, 2 * T), F32), ((96, 2 * T), BF), ((8, 128), F32)],
        meta, mine, sums, got3, dbs, ym, yo, out=True)

    b = d % 2

    def quarters(keep, gx, gz, gxz):
        rx = swap(gx, 1, 0, 0)
        pairs = [(i * 2 + k, (i ^ 1) * 2 + 1 - k) for i in range(dp_size) for k in range(2)]
        rxz = lax.ppermute(gxz, ("dp", "head"), pairs)
        rz = swap_dp(gz, 1, dp_size)
        return (keep + rx.astype(F32) + rz.astype(F32) + rxz.astype(F32)).astype(BF)

    def halves(keep, his, gx):
        rx = swap(gx, 1, 0, 0)
        n = keep.shape[0]
        his, keep = his + rx[n:].astype(F32), keep + rx[:n].astype(F32)
        his = his.astype(BF)
        rz = swap_dp(his, 1, dp_size)
        return (keep + rz.astype(F32)).astype(BF)

    def finish(sm):
        dist = 2
        while dist < dp_size:
            got = swap_dp(sm, dist, dp_size)
            sm = (sm.astype(F32) + got.astype(F32)).astype(BF)
            dist *= 2
        return sm, swap_dp(sm, 1, dp_size)

    def both(sm, so, axis=0):
        lo, hi = pick(b == 0, sm, so)
        return jnp.concatenate([lo, hi], axis=axis).astype(F32)

    gd = both(*finish(quarters(*gd4)))
    gu = both(*finish(quarters(*gu4)), axis=1)
    o_own, o_oth = finish(halves(*go3))
    gq = both(*finish(halves(*gq3)))
    gq = gq.reshape(3, hc, HALF).transpose(2, 0, 1)
    n = hc // 2
    go = both(o_own[:n], o_oth[:n])
    cols = block_in.shape[1]
    dist = 1
    while dist < dp_size:
        vsum = vsum + swap_dp(vsum, dist, dp_size)
        dist *= 2
    *v6, qv = kernel_call(
        k_vectors, [((1, cols), F32)] * 6 + [((2, hc), F32)], meta, o_own, o_oth, vsum, out=True)
    n1g, n1b, ob, n2g, n2b, db = (v.reshape(cols) for v in v6)
    return (y_out.T, grad_in.T, n1g, n1b, gq, qv, go, ob, n2g, n2b, gu[:HALF], gu[HALF], gd, db)


def solution(mesh):
    dp_size = mesh.shape["dp"]
    hw = ("head", "width")

    def run(*args):
        return body(dp_size, *args)

    return jax.shard_map(
        run,
        mesh=mesh,
        in_specs=(
            P("dp", hw), P(("dp", "head")), P("dp"), P(hw), P(hw), P("head", None, "width"),
            P(None, "width"), P("width", "head"), P(hw), P(hw), P(hw), P("head", "width"),
            P("width"), P("width", "head"), P(hw), P("dp", hw),
        ),
        out_specs=(
            P("dp", hw), P("dp", hw), P(hw), P(hw), P("head", None, "width"), P(None, "width"),
            P("width", "head"), P(hw), P(hw), P(hw), P("head", "width"), P("width"),
            P("width", "head"), P(hw),
        ),
        check_vma=False,
    )
```
